32 devices in a mesh: row: 4 (over z), col: 8 (over y, x, core).
Axes of the slice: x: 2, y: 2, z: 4, core: 2. Of those that a mesh axis runs over, the one named last changes fastest.
Arguments:
- tokens: bfloat16 [128, 8192], P('col', 'row'), may hold values from -6 to 6
- cotangent: bfloat16 [128, 8192], P('col', 'row'), may hold values from -6 to 6
- up_weight: bfloat16 [8192, 32768], P('row', 'col'), may hold values from -0.125 to 0.125
- down_weight: bfloat16 [32768, 8192], P('col', 'row'), may hold values from -0.0625 to 0.0625
- block_index: int32 [64, 96], replicated, may hold values from 0 to 256, as said below
Outputs:
- input_grad: bfloat16 [128, 8192], P('col', 'row')
- up_grad: bfloat16 [8192, 32768], P('row', 'col')
- down_grad: bfloat16 [32768, 8192], P('col', 'row')
The draws below stay inside these ranges and needn't reach their ends.
Inputs may be any that keep to these rules, and one draw needn't show every extreme that they name: `block_index`: row i lists distinct block columns in rising order, then the value 256 as padding up to 96 entries; each row keeps 32 to 96 blocks, and some row keeps exactly 96.
All inputs are finite; a program needn't handle non-finite values.
Results may differ from the reference program's by a relative error of at most 0.005.
Values may be sent and summed in bfloat16 or wider, within the bound.
No kernel may reach another device: no remote copies, remote signals or barrier semaphores. Data moves between devices by JAX's collectives and lax.ppermute only.
A program may use at most 256 MiB of HBM per device.

```python
import jax
import jax.numpy as jnp
from jax import lax

D = 8192
F = 32768
BLOCK = 128
KMAX = 96
KMIN = 32
TOKENS = 128
DB = 64
FB = 256


def shuffled(seed_key):
    return jax.random.permutation(seed_key, FB)


def draw_block_index(key, part):
    key_count, key_perm, key_row = jax.random.split(key, 3)
    counts = jax.random.randint(key_count, (DB,), KMIN, KMAX + 1)
    chosen = jax.random.randint(key_row, (), 0, DB)
    counts = jnp.where(jnp.arange(DB) == chosen, KMAX, counts)
    orders = jax.vmap(shuffled)(jax.random.split(key_perm, DB))
    leading = orders[:, :KMAX].astype(jnp.int32)
    places = jnp.arange(KMAX)[None, :]
    listed = jnp.where(places < counts[:, None], leading, FB)
    return jnp.sort(listed, axis=1).astype(jnp.int32)


def levels(rng, shape, cuts, low, largest):
    def one(position, blocks):
        steps = jax.random.uniform(jax.random.fold_in(jax.random.fold_in(rng, 6), position), (blocks,), jnp.float32, low / len(cuts), largest / len(cuts))
        return jnp.repeat(jnp.exp(steps), shape[position] // blocks).reshape((-1,) + (1,) * (len(shape) - position - 1))

    level = one(*cuts[0])
    for cut in cuts[1:]:
        level = level * one(*cut)
    return level


def centred(rng, extent, scale, bound, pieces=(), kind=jnp.bfloat16):
    loudness = levels(rng, extent, pieces, -0.22, 0.18) if pieces else 1.0
    result = jax.random.normal(rng, extent, jnp.float32) * scale * loudness
    return jnp.minimum(jnp.maximum(result, -bound), bound).astype(kind)


def setup_inputs(seed: int = 0) -> dict:
    seeds = jax.random.split(jax.random.key(seed), 6)
    tokens = centred(seeds[0], (TOKENS, D), 1.0, 6.0, ((0, 8), (1, 4)))
    cotangent = centred(seeds[1], (TOKENS, D), 1.0, 6.0, ((0, 8), (1, 4)))
    up_weight = centred(seeds[2], (D, F), (D // 4) ** -0.5, 0.125, ((0, 4), (1, 8)))
    down_weight = centred(seeds[3], (F, D), (F // 4) ** -0.5, 0.0625, ((0, 8), (1, 4)))
    block_index = draw_block_index(jax.random.fold_in(seeds[5], 71), 0)
    return {"tokens": tokens, "cotangent": cotangent, "up_weight": up_weight, "down_weight": down_weight, "block_index": block_index}


def reference(tokens, cotangent, up_weight, down_weight, block_index):
    columns = jnp.arange(FB, dtype=jnp.int32)
    block_hits = jnp.any(block_index[:, :, None] == columns[None, None, :], axis=1)
    mask_half = block_hits.astype(jnp.bfloat16)
    mask_full = block_hits.astype(jnp.float32)
    masked_up = (up_weight.reshape(DB, BLOCK, FB, BLOCK) * mask_half[:, None, :, None]).reshape(D, F)
    masked_down = (down_weight.reshape(FB, BLOCK, DB, BLOCK) * mask_half.T[:, None, :, None]).reshape(F, D)
    hidden = jnp.dot(tokens, masked_up, preferred_element_type=jnp.float32)
    act_grad = lax.dot_general(cotangent, masked_down, (((1,), (1,)), ((), ())), preferred_element_type=jnp.float32)
    activated = jax.nn.gelu(hidden).astype(jnp.bfloat16)
    _, pullback = jax.vjp(jax.nn.gelu, hidden)
    hidden_grad = pullback(act_grad)[0].astype(jnp.bfloat16)
    down_sum = lax.dot_general(activated, cotangent, (((0,), (0,)), ((), ())), preferred_element_type=jnp.float32)
    down_grad = (down_sum.reshape(FB, BLOCK, DB, BLOCK) * mask_full.T[:, None, :, None]).reshape(F, D).astype(jnp.bfloat16)
    up_sum = lax.dot_general(tokens, hidden_grad, (((0,), (0,)), ((), ())), preferred_element_type=jnp.float32)
    up_grad = (up_sum.reshape(DB, BLOCK, FB, BLOCK) * mask_full[:, None, :, None]).reshape(D, F).astype(jnp.bfloat16)
    input_grad = lax.dot_general(hidden_grad, masked_up, (((1,), (1,)), ((), ())), preferred_element_type=jnp.float32)
    return (input_grad.astype(jnp.bfloat16), up_grad, down_grad)
```

```python
import functools

import jax
import jax.numpy as jnp
from jax import lax
from jax.experimental import pallas as pl
from jax.experimental.pallas import tpu as pltpu
from jax.sharding import PartitionSpec as P


BLOCK = 128
SUB = 16
PAIR = 2
VMEM_LIMIT = 56 * 1024 * 1024
SHARES = (3, 4, 4, 3, 2)
ROOT = 0.7978845608028654
CUBE = 0.044715


def chunk_steps(steps):
    total = sum(SHARES)
    edges = [0]
    run = 0
    for share in SHARES:
        run += share
        edge = (run * steps) // total
        if edge > edges[-1]:
            edges.append(edge)
    return [(a, b - a) for a, b in zip(edges[:-1], edges[1:])]


def tile_mask(block_index, row_blocks, col_blocks):
    row_place = lax.axis_index("row")
    col_place = lax.axis_index("col")
    own_rows = lax.dynamic_slice_in_dim(block_index, row_place * row_blocks, row_blocks, 0)
    own_cols = col_place * col_blocks + jnp.arange(col_blocks, dtype=jnp.int32)
    return jnp.any(own_rows[:, :, None] == own_cols[None, None, :], axis=1)


def masked(block, mask):
    groups = mask.shape[0]
    width = block.shape[1]
    tiled = block.reshape(groups, BLOCK // SUB, SUB, width) * mask[:, None]
    return tiled.reshape(groups * BLOCK, width)


def dot(a, b, dims=((1,), (0,))):
    return lax.dot_general(a, b, (dims, ((), ())), preferred_element_type=jnp.float32)


def forward_kernel(pair_ref, up_ref, down_ref, mu_ref, md_ref, own_ref, send_ref):
    up = masked(up_ref[...], mu_ref[...])
    hidden = dot(pair_ref[0], up)
    own_ref[0] = hidden
    send_ref[0] = hidden.astype(send_ref.dtype)
    down = masked(down_ref[...], md_ref[...])
    grad = dot(pair_ref[1], down, ((1,), (1,)))
    own_ref[1] = grad
    send_ref[1] = grad.astype(send_ref.dtype)


def forward(pair, up, down, mu, md, first, count, width):
    _, tokens, feats = pair.shape
    blocks = width // BLOCK
    part = pl.BlockSpec((2, tokens, width), lambda j: (0, 0, j))
    return pl.pallas_call(
        forward_kernel,
        grid=(count,),
        in_specs=[
            pl.BlockSpec((2, tokens, feats), lambda j: (0, 0, 0)),
            pl.BlockSpec((feats, width), lambda j: (0, first + j)),
            pl.BlockSpec((width, feats), lambda j: (first + j, 0)),
            pl.BlockSpec((feats // BLOCK, SUB, width), lambda j: (0, 0, first + j)),
            pl.BlockSpec((blocks, SUB, feats), lambda j: (first + j, 0, 0)),
        ],
        out_specs=[part, part],
        out_shape=[
            jax.ShapeDtypeStruct((2, tokens, count * width), jnp.float32),
            jax.ShapeDtypeStruct((2, tokens, count * width), jnp.bfloat16),
        ],
        compiler_params=pltpu.CompilerParams(vmem_limit_bytes=VMEM_LIMIT),
        cost_estimate=pl.CostEstimate(
            flops=4 * tokens * feats * width * count,
            bytes_accessed=4 * feats * width * count + 4 * tokens * feats,
            transcendentals=0,
        ),
        name="forward",
    )(pair, up, down, mu, md)


def finish(v, g):
    square = v * v
    t = jnp.tanh(v * (ROOT + (ROOT * CUBE) * square))
    half = 0.5 + 0.5 * t
    slope = half + (0.5 * v) * ((1.0 - t) * (1.0 + t)) * (ROOT + (3.0 * ROOT * CUBE) * square)
    return v * half, g * slope


def inner(own, came, up, mu, state, first, count, width):
    _, tokens, chunk = own.shape
    feats = up.shape[0]
    have = state is not None
    n_came = len(came)
    rows = tokens // 2

    def body(*refs):
        own_ref, came_refs, up_ref, mu_ref = refs[0], refs[1:1 + n_came], refs[1 + n_came], refs[2 + n_came]
        act_ref, hgrad_ref, lo_ref, hi_ref = refs[-4:]

        @pl.when(pl.program_id(0) == 0)
        def _():
            lo_ref[...] = refs[3 + n_came][...] if have else jnp.zeros_like(lo_ref)
            hi_ref[...] = refs[4 + n_came][...] if have else jnp.zeros_like(hi_ref)

        def total(k):
            value = own_ref[k]
            for ref in came_refs:
                value += ref[k].astype(jnp.float32)
            return value

        act, grad = finish(total(0), total(1))
        hgrad = grad.astype(jnp.bfloat16)
        act_ref[...] = act.astype(jnp.bfloat16)
        hgrad_ref[...] = hgrad
        band = min(feats, 4 * BLOCK)
        for b in range(feats // band):
            cut = slice(b * band, (b + 1) * band)
            part = dot(hgrad, masked(up_ref[cut, :], mu_ref[b * (band // BLOCK):(b + 1) * (band // BLOCK)]), ((1,), (1,)))
            lo_ref[:, cut] += part[:rows]
            hi_ref[:, cut] += part[rows:]

    part = pl.BlockSpec((2, tokens, width), lambda j: (0, 0, j))
    half_spec = pl.BlockSpec((rows, feats), lambda j: (0, 0))
    out = pl.BlockSpec((tokens, width), lambda j: (0, j))
    return pl.pallas_call(
        body,
        grid=(count,),
        in_specs=[
            *([part] * (1 + n_came)),
            pl.BlockSpec((feats, width), lambda j: (0, first + j)),
            pl.BlockSpec((feats // BLOCK, SUB, width), lambda j: (0, 0, first + j)),
            *([half_spec] * (2 if have else 0)),
        ],
        out_specs=[out, out, half_spec, half_spec],
        out_shape=[
            jax.ShapeDtypeStruct((tokens, chunk), jnp.bfloat16),
            jax.ShapeDtypeStruct((tokens, chunk), jnp.bfloat16),
            jax.ShapeDtypeStruct((rows, feats), jnp.float32),
            jax.ShapeDtypeStruct((rows, feats), jnp.float32),
        ],
        compiler_params=pltpu.CompilerParams(vmem_limit_bytes=VMEM_LIMIT),
        cost_estimate=pl.CostEstimate(
            flops=2 * tokens * feats * chunk,
            bytes_accessed=2 * feats * chunk + 8 * tokens * feats,
            transcendentals=tokens * chunk,
        ),
        name="inner",
    )(own, *came, up, mu, *(state or ()))


def weight_grads(tokt, pair, act, hgrad, mu, md, grads, units, first, count, width):
    _, tokens, feats = pair.shape
    blocks = width // BLOCK
    have = grads is not None

    def body(*refs):
        tokt_ref, cot_ref, act_ref, hgrad_ref, mu_ref, md_ref = refs[:6]
        upg_ref, dng_ref = refs[-2:]
        hgrad = hgrad_ref[...]
        act_t = act_ref[...].astype(jnp.float32).T.astype(jnp.bfloat16)
        band = min(feats, 4 * BLOCK)
        for b in range(feats // band):
            cut = slice(b * band, (b + 1) * band)
            mask = mu_ref[b * (band // BLOCK):(b + 1) * (band // BLOCK)]
            upg_ref[cut, :] = masked(dot(tokt_ref[cut, :], hgrad).astype(jnp.bfloat16), mask)
            dng_ref[:, cut] = masked(dot(act_t, cot_ref[0, :, cut]).astype(jnp.bfloat16), md_ref[:, :, cut])

    part = pl.BlockSpec((tokens, width), lambda j: (0, j))
    any_spec = pl.BlockSpec(memory_space=pl.ANY)
    return pl.pallas_call(
        body,
        grid=(count,),
        in_specs=[
            pl.BlockSpec((feats, tokens), lambda j: (0, 0)),
            pl.BlockSpec((1, tokens, feats), lambda j: (1, 0, 0)),
            part,
            part,
            pl.BlockSpec((feats // BLOCK, SUB, width), lambda j: (0, 0, first + j)),
            pl.BlockSpec((blocks, SUB, feats), lambda j: (first + j, 0, 0)),
            *([any_spec] * (2 if have else 0)),
        ],
        out_specs=[
            pl.BlockSpec((feats, width), lambda j: (0, first + j)),
            pl.BlockSpec((width, feats), lambda j: (first + j, 0)),
        ],
        out_shape=[
            jax.ShapeDtypeStruct((feats, units), jnp.bfloat16),
            jax.ShapeDtypeStruct((units, feats), jnp.bfloat16),
        ],
        input_output_aliases={6: 0, 7: 1} if have else {},
        compiler_params=pltpu.CompilerParams(vmem_limit_bytes=VMEM_LIMIT),
        cost_estimate=pl.CostEstimate(
            flops=4 * tokens * feats * width * count,
            bytes_accessed=4 * feats * width * count + 4 * tokens * feats,
            transcendentals=0,
        ),
        name="weight_grads",
    )(tokt, pair, act, hgrad, mu, md, *(grads or ()))


def xor_pairs(n, bits):
    return [(i, i ^ bits) for i in range(n)]


def gather_tokens(x, n, masks):
    if n == 1:
        return x, masks
    parts = [x] + [lax.ppermute(x, "col", xor_pairs(n, s)) for s in range(2, n, 2)]
    half = jnp.concatenate(parts, axis=1)
    half, masks = lax.optimization_barrier((half, masks))
    return jnp.concatenate([half, lax.ppermute(half, "col", xor_pairs(n, 1))], axis=1), masks


def scatter_tokens(lo, hi, n):
    mine = lo + lax.ppermute(hi, "col", xor_pairs(n, 1))
    rows = 2 * mine.shape[0] // n
    send = mine[rows:].astype(jnp.bfloat16)
    out = mine[:rows]
    for k, s in enumerate(range(2, n, 2)):
        came = lax.ppermute(send[k * rows:(k + 1) * rows], "col", xor_pairs(n, s))
        out = out + came.astype(jnp.float32)
    return out


def shift(x, pairs):
    return lax.ppermute(x, "row", pairs)


def local(rows, cols, tokens, cotangent, up_weight, down_weight, block_index):
    feats, units = up_weight.shape
    row_blocks = feats // BLOCK
    col_blocks = units // BLOCK
    hits = tile_mask(block_index, row_blocks, col_blocks).astype(jnp.bfloat16)
    mu = jnp.broadcast_to(hits[:, None, :, None], (row_blocks, SUB, col_blocks, BLOCK)).reshape(row_blocks, SUB, units)
    md = jnp.broadcast_to(hits.T[:, None, :, None], (col_blocks, SUB, row_blocks, BLOCK)).reshape(col_blocks, SUB, feats)
    pair, (mu, md) = gather_tokens(jnp.stack([tokens, cotangent]), cols, (mu, md))
    tokt = pair[0].T
    width = PAIR * BLOCK
    plan = chunk_steps(units // width)
    right = rows // 2
    sums = []
    for first, count in plan:
        own, near = forward(pair, up_weight, down_weight, mu, md, first, count, width)
        came = []
        for k in range(right - 1):
            came.append(shift(near, [(k, k + 1), (rows - 1 - k, rows - 2 - k)]))
            near = (own + sum(x.astype(jnp.float32) for x in came)).astype(jnp.bfloat16)
        came.append(shift(near, [(right - 1, right), (right, right - 1)]))
        out = own + came[-1].astype(jnp.float32)
        for k in reversed(range(right - 1)):
            far = shift(out.astype(jnp.bfloat16), [(k + 1, k), (rows - 2 - k, rows - 1 - k)])
            came.append(far)
            out = out + far.astype(jnp.float32)
        sums.append((own, came))
    state = grads = None
    for c, (first, count) in enumerate(plan):
        act, hgrad, *state = inner(*sums[c], up_weight, mu, state, first, count, width)
        grads = weight_grads(tokt, pair, act, hgrad, mu, md, grads, units, first, count, width)
    input_grad = scatter_tokens(*state, cols)
    return (input_grad.astype(jnp.bfloat16), *grads)


def whole(rows, cols, *arrays):
    return local(rows, cols, *arrays)


def solution(mesh):
    return jax.shard_map(
        functools.partial(whole, mesh.shape["row"], mesh.shape["col"]),
        mesh=mesh,
        in_specs=(P("col", "row"), P("col", "row"), P("row", "col"), P("col", "row"), P()),
        out_specs=(P("col", "row"), P("row", "col"), P("col", "row")),
        check_vma=False,
    )
```

```python
import functools

import jax
import jax.numpy as jnp
from jax import lax
from jax.experimental import pallas as pl
from jax.experimental.pallas import tpu as pltpu
from jax.sharding import PartitionSpec as P


BLOCK = 128
SUB = 16
PAIR = 2
VMEM_LIMIT = 24 * 1024 * 1024
PARAMS = pltpu.CompilerParams(vmem_limit_bytes=VMEM_LIMIT)
SHARES = (3, 5, 5, 3)
GROUPS = (1, 1, 1, 1)
LATE = 1
BAND = 4
ROOT = 0.7978845608028654
CUBE = 0.044715


def chunk_steps(steps):
    total = sum(SHARES)
    edges = [0]
    run = 0
    for share in SHARES:
        run += share
        edge = (run * steps) // total
        if edge > edges[-1]:
            edges.append(edge)
    return [(a, b - a) for a, b in zip(edges[:-1], edges[1:])]


def tile_mask(block_index, row_blocks, col_blocks):
    row_place = lax.axis_index("row")
    col_place = lax.axis_index("col")
    own_rows = lax.dynamic_slice_in_dim(block_index, row_place * row_blocks, row_blocks, 0)
    own_cols = col_place * col_blocks + jnp.arange(col_blocks, dtype=jnp.int32)
    return jnp.any(own_rows[:, :, None] == own_cols[None, None, :], axis=1)


def masked(block, mask_ref, first, cut=slice(None)):
    rows, width = block.shape
    parts = []
    for g in range(rows // BLOCK):
        row = jnp.broadcast_to(mask_ref[first + g:first + g + 1, cut], (SUB, width)).astype(block.dtype)
        part = block[g * BLOCK:(g + 1) * BLOCK].reshape(BLOCK // SUB, SUB, width) * row[None]
        parts.append(part.reshape(BLOCK, width))
    return jnp.concatenate(parts, axis=0) if len(parts) > 1 else parts[0]


def dot(a, b, dims=((1,), (0,))):
    return lax.dot_general(a, b, (dims, ((), ())), preferred_element_type=jnp.float32)


def forward(pair, up, down, mu, md, first, counts, width):
    _, tokens, feats = pair.shape
    blocks = width // BLOCK
    steps = sum(counts)
    edges = [sum(counts[:k]) for k in range(len(counts))]

    def body(pair_ref, up_ref, down_ref, mu_ref, md_ref, *out_refs):
        step = pl.program_id(0)
        hidden = dot(pair_ref[0], masked(up_ref[...], mu_ref, 0))
        grad = dot(pair_ref[1], masked(down_ref[...], md_ref.at[0], 0), ((1,), (1,)))
        for k, (edge, count) in enumerate(zip(edges, counts)):
            def put(k=k):
                own_ref, send_ref = out_refs[2 * k:2 * k + 2]
                own_ref[0] = hidden
                own_ref[1] = grad
                send_ref[0] = hidden.astype(send_ref.dtype)
                send_ref[1] = grad.astype(send_ref.dtype)

            if len(counts) == 1:
                put()
            else:
                pl.when((step >= edge) & (step < edge + count))(put)

    def part(edge, count):
        return pl.BlockSpec((2, tokens, width), lambda j: (0, 0, jnp.clip(j - edge, 0, count - 1)))

    out_specs, out_shape = [], []
    for edge, count in zip(edges, counts):
        for kind in (jnp.float32, jnp.bfloat16):
            out_specs.append(part(edge, count))
            out_shape.append(jax.ShapeDtypeStruct((2, tokens, count * width), kind))
    return pl.pallas_call(
        body,
        grid=(steps,),
        in_specs=[
            pl.BlockSpec((2, tokens, feats), lambda j: (0, 0, 0)),
            pl.BlockSpec((feats, width), lambda j: (0, first + j)),
            pl.BlockSpec((width, feats), lambda j: (first + j, 0)),
            pl.BlockSpec((feats // BLOCK, width), lambda j: (0, first + j)),
            pl.BlockSpec((1, blocks, feats), lambda j: (first + j, 0, 0)),
        ],
        out_specs=out_specs,
        out_shape=out_shape,
        compiler_params=PARAMS,
        cost_estimate=pl.CostEstimate(
            flops=4 * tokens * feats * width * steps,
            bytes_accessed=4 * feats * width * steps + 4 * tokens * feats,
            transcendentals=0,
        ),
        name="forward",
    )(pair, up, down, mu, md)


def finish(v, g):
    square = v * v
    t = jnp.tanh(v * (ROOT + (ROOT * CUBE) * square))
    half = 0.5 + 0.5 * t
    slope = half + (0.5 * v) * ((1.0 - t) * (1.0 + t)) * (ROOT + (3.0 * ROOT * CUBE) * square)
    return v * half, g * slope


def chunk_kernel(own, came, up, mu, state, grads, weights, first, count, width):
    _, tokens, chunk = own.shape
    feats, units = up.shape
    blocks = width // BLOCK
    rows = tokens // 2
    n_came = len(came)

    def body(*refs):
        refs = list(refs)
        own_ref = refs.pop(0)
        came_refs = [refs.pop(0) for _ in range(n_came)]
        up_ref, mu_ref = refs.pop(0), refs.pop(0)
        lo_in, hi_in = (refs.pop(0), refs.pop(0)) if state else (None, None)
        if weights:
            tokt_ref, cot_ref, md_ref = refs[:3]
        lo_ref, hi_ref, one_ref, two_ref = refs[-4:]

        @pl.when(pl.program_id(0) == 0)
        def _():
            lo_ref[...] = lo_in[...] if state else jnp.zeros_like(lo_ref)
            hi_ref[...] = hi_in[...] if state else jnp.zeros_like(hi_ref)

        def total(k):
            value = own_ref[k]
            for ref in came_refs:
                value += ref[k].astype(jnp.float32)
            return value

        act, grad = finish(total(0), total(1))
        hgrad = grad.astype(jnp.bfloat16)
        if weights:
            act_t = act.T.astype(jnp.bfloat16)
        else:
            one_ref[...] = act.astype(jnp.bfloat16)
            two_ref[...] = hgrad
        band = min(feats, BAND * BLOCK)
        for b in range(feats // band):
            cut = slice(b * band, (b + 1) * band)
            at = b * (band // BLOCK)
            part = dot(hgrad, masked(up_ref[cut, :], mu_ref, at), ((1,), (1,)))
            lo_ref[:, cut] += part[:rows]
            hi_ref[:, cut] += part[rows:]
            if weights:
                one_ref[cut, :] = masked(dot(tokt_ref[cut, :], hgrad).astype(jnp.bfloat16), mu_ref, at)
                two_ref[:, cut] = masked(dot(act_t, cot_ref[0, :, cut]).astype(jnp.bfloat16), md_ref.at[0], 0, cut)

    part = pl.BlockSpec((2, tokens, width), lambda j: (0, 0, j))
    half_spec = pl.BlockSpec((rows, feats), lambda j: (0, 0))
    half_shape = jax.ShapeDtypeStruct((rows, feats), jnp.float32)
    in_specs = [
        *([part] * (1 + n_came)),
        pl.BlockSpec((feats, width), lambda j: (0, first + j)),
        pl.BlockSpec((feats // BLOCK, width), lambda j: (0, first + j)),
        *([half_spec] * (2 if state else 0)),
    ]
    operands = [own, *came, up, mu, *(state or ())]
    aliases = {}
    if weights:
        in_specs += weight_in_specs(tokens, feats, blocks, first)
        operands += weights
        if grads:
            aliases = {len(operands): 2, len(operands) + 1: 3}
            in_specs += [pl.BlockSpec(memory_space=pl.ANY)] * 2
            operands += grads
        out_specs, out_shape = weight_outs(feats, units, first, width)
    else:
        out_specs = [pl.BlockSpec((tokens, width), lambda j: (0, j))] * 2
        out_shape = [jax.ShapeDtypeStruct((tokens, chunk), jnp.bfloat16)] * 2
    times = 3 if weights else 1
    return pl.pallas_call(
        body,
        grid=(count,),
        in_specs=in_specs,
        out_specs=[half_spec, half_spec, *out_specs],
        out_shape=[half_shape, half_shape, *out_shape],
        input_output_aliases=aliases,
        compiler_params=PARAMS,
        cost_estimate=pl.CostEstimate(
            flops=2 * times * tokens * feats * chunk,
            bytes_accessed=2 * times * feats * chunk + 8 * tokens * feats,
            transcendentals=tokens * chunk,
        ),
        name="chunk",
    )(*operands)


def weight_in_specs(tokens, feats, blocks, first):
    return [
        pl.BlockSpec((feats, tokens), lambda j: (0, 0)),
        pl.BlockSpec((1, tokens, feats), lambda j: (1, 0, 0)),
        pl.BlockSpec((1, blocks, feats), lambda j: (first + j, 0, 0)),
    ]


def weight_outs(feats, units, first, width):
    specs = [
        pl.BlockSpec((feats, width), lambda j: (0, first + j)),
        pl.BlockSpec((width, feats), lambda j: (first + j, 0)),
    ]
    return specs, [pltpu.HBM((feats, units), jnp.bfloat16), pltpu.HBM((units, feats), jnp.bfloat16)]


def weight_grads(act, hgrad, mu, weights, grads, units, first, count, width):
    tokens, feats = weights[1].shape[1:]

    def body(tokt_ref, cot_ref, md_ref, act_ref, hgrad_ref, mu_ref, *refs):
        upg_ref, dng_ref = refs[-2:]
        hgrad = hgrad_ref[...]
        act_t = act_ref[...].astype(jnp.float32).T.astype(jnp.bfloat16)
        band = min(feats, BAND * BLOCK)
        for b in range(feats // band):
            cut = slice(b * band, (b + 1) * band)
            upg_ref[cut, :] = masked(dot(tokt_ref[cut, :], hgrad).astype(jnp.bfloat16), mu_ref, b * (band // BLOCK))
            dng_ref[:, cut] = masked(dot(act_t, cot_ref[0, :, cut]).astype(jnp.bfloat16), md_ref.at[0], 0, cut)

    part = pl.BlockSpec((tokens, width), lambda j: (0, j))
    any_spec = pl.BlockSpec(memory_space=pl.ANY)
    out_specs, out_shape = weight_outs(feats, units, first, width)
    return pl.pallas_call(
        body,
        grid=(count,),
        in_specs=[
            *weight_in_specs(tokens, feats, width // BLOCK, first),
            part,
            part,
            pl.BlockSpec((feats // BLOCK, width), lambda j: (0, first + j)),
            *([any_spec] * (2 if grads else 0)),
        ],
        out_specs=out_specs,
        out_shape=out_shape,
        input_output_aliases={6: 0, 7: 1} if grads else {},
        compiler_params=PARAMS,
        cost_estimate=pl.CostEstimate(
            flops=4 * tokens * feats * width * count,
            bytes_accessed=4 * feats * width * count + 4 * tokens * feats,
            transcendentals=0,
        ),
        name="weight_grads",
    )(*weights, act, hgrad, mu, *(grads or ()))


def xor_pairs(n, bits):
    return [(i, i ^ bits) for i in range(n)]


def gather_tokens(x, n, masks):
    if n == 1:
        return x, masks
    parts = [x] + [lax.ppermute(x, "col", xor_pairs(n, s)) for s in range(2, n, 2)]
    half = jnp.concatenate(parts, axis=1)
    half, masks = lax.optimization_barrier((half, masks))
    return jnp.concatenate([half, lax.ppermute(half, "col", xor_pairs(n, 1))], axis=1), masks


def scatter_tokens(lo, hi, n):
    mine = lo + lax.ppermute(hi, "col", xor_pairs(n, 1))
    rows = 2 * mine.shape[0] // n
    send = mine[rows:].astype(jnp.bfloat16)
    out = mine[:rows]
    for k, s in enumerate(range(2, n, 2)):
        came = lax.ppermute(send[k * rows:(k + 1) * rows], "col", xor_pairs(n, s))
        out = out + came.astype(jnp.float32)
    return out


def shift(x, pairs):
    return lax.ppermute(x, "row", pairs)


def local(rows, cols, tokens, cotangent, up_weight, down_weight, block_index):
    feats, units = up_weight.shape
    row_blocks = feats // BLOCK
    col_blocks = units // BLOCK
    hits = tile_mask(block_index, row_blocks, col_blocks).astype(jnp.float32)
    width = PAIR * BLOCK
    mu = jnp.repeat(hits, BLOCK, axis=1)
    md = jnp.repeat(hits.T, BLOCK, axis=1).reshape(units // width, PAIR, feats)
    pair, (mu, md) = gather_tokens(jnp.stack([tokens, cotangent]), cols, (mu, md))
    up_weight, down_weight = (pltpu.with_memory_space_constraint(w, pltpu.HBM) for w in (up_weight, down_weight))
    weights = [pair[0].T, pair, md]
    plan = chunk_steps(units // width)
    owns = []
    while len(owns) < len(plan):
        group = plan[len(owns):len(owns) + GROUPS[min(len(owns), len(GROUPS) - 1)]]
        outs = forward(pair, up_weight, down_weight, mu, md, group[0][0], [n for _, n in group], width)
        owns += list(zip(outs[::2], outs[1::2]))
    right = rows // 2
    sums = []
    for own, near in owns:
        came = []
        for k in range(right - 1):
            came.append(shift(near, [(k, k + 1), (rows - 1 - k, rows - 2 - k)]))
            near = (own + sum(x.astype(jnp.float32) for x in came)).astype(jnp.bfloat16)
        came.append(shift(near, [(right - 1, right), (right, right - 1)]))
        out = own + came[-1].astype(jnp.float32)
        for k in reversed(range(right - 1)):
            far = shift(out.astype(jnp.bfloat16), [(k + 1, k), (rows - 2 - k, rows - 1 - k)])
            came.append(far)
            out = out + far.astype(jnp.float32)
        sums.append((own, came))
    state = grads = None
    late = []
    for c, (first, count) in enumerate(plan):
        whole_chunk = c + LATE < len(plan)
        *state, one, two = chunk_kernel(
            *sums[c], up_weight, mu, state, grads, weights if whole_chunk else None, first, count, width
        )
        if whole_chunk:
            grads = [one, two]
        else:
            late.append((c, first, count, one, two))
    for c, first, count, act, hgrad in late:
        grads = weight_grads(act, hgrad, mu, weights, grads, units, first, count, width)
    input_grad = scatter_tokens(*state, cols)
    return (input_grad.astype(jnp.bfloat16), *grads)


def whole(rows, cols, *arrays):
    return local(rows, cols, *arrays)


def solution(mesh):
    return jax.shard_map(
        functools.partial(whole, mesh.shape["row"], mesh.shape["col"]),
        mesh=mesh,
        in_specs=(P("col", "row"), P("col", "row"), P("row", "col"), P("col", "row"), P()),
        out_specs=(P("col", "row"), P("row", "col"), P("col", "row")),
        check_vma=False,
    )
```

```python
import functools

import jax
import jax.numpy as jnp
from jax import lax
from jax.experimental import pallas as pl
from jax.experimental.pallas import tpu as pltpu
from jax.sharding import PartitionSpec as P


BLOCK = 128
SUB = 16
PAIR = 2
VMEM_LIMIT = 20 * 1024 * 1024
PARAMS = pltpu.CompilerParams(vmem_limit_bytes=VMEM_LIMIT)
SHARES = (3, 4, 4, 4, 1)
GROUPS = (1, 1, 1, 1, 1)
LATE = 1
BAND = 4
ROOT = 0.7978845608028654
CUBE = 0.044715


def chunk_steps(steps):
    total = sum(SHARES)
    edges = [0]
    run = 0
    for share in SHARES:
        run += share
        edge = (run * steps) // total
        if edge > edges[-1]:
            edges.append(edge)
    return [(a, b - a) for a, b in zip(edges[:-1], edges[1:])]


def tile_mask(block_index, row_blocks, col_blocks):
    row_place = lax.axis_index("row")
    col_place = lax.axis_index("col")
    own_rows = lax.dynamic_slice_in_dim(block_index, row_place * row_blocks, row_blocks, 0)
    own_cols = col_place * col_blocks + jnp.arange(col_blocks, dtype=jnp.int32)
    return jnp.any(own_rows[:, :, None] == own_cols[None, None, :], axis=1)


def masked(block, mask_ref, first, cut=slice(None)):
    rows, width = block.shape
    parts = []
    for g in range(rows // BLOCK):
        row = jnp.broadcast_to(mask_ref[first + g:first + g + 1, cut], (SUB, width)).astype(block.dtype)
        part = block[g * BLOCK:(g + 1) * BLOCK].reshape(BLOCK // SUB, SUB, width) * row[None]
        parts.append(part.reshape(BLOCK, width))
    return jnp.concatenate(parts, axis=0) if len(parts) > 1 else parts[0]


def dot(a, b, dims=((1,), (0,))):
    return lax.dot_general(a, b, (dims, ((), ())), preferred_element_type=jnp.float32)


def forward(pair, up, down, mu, md, first, counts, width):
    _, tokens, feats = pair.shape
    blocks = width // BLOCK
    steps = sum(counts)
    edges = [sum(counts[:k]) for k in range(len(counts))]

    def body(pair_ref, up_ref, down_ref, mu_ref, md_ref, *out_refs):
        step = pl.program_id(0)
        hidden = dot(pair_ref[0], masked(up_ref[...], mu_ref, 0))
        grad = dot(pair_ref[1], masked(down_ref[...], md_ref.at[0], 0), ((1,), (1,)))
        for k, (edge, count) in enumerate(zip(edges, counts)):
            def put(k=k):
                own_ref, send_ref = out_refs[2 * k:2 * k + 2]
                own_ref[0] = hidden
                own_ref[1] = grad
                send_ref[0] = hidden.astype(send_ref.dtype)
                send_ref[1] = grad.astype(send_ref.dtype)

            if len(counts) == 1:
                put()
            else:
                pl.when((step >= edge) & (step < edge + count))(put)

    def part(edge, count):
        return pl.BlockSpec((2, tokens, width), lambda j: (0, 0, jnp.clip(j - edge, 0, count - 1)))

    out_specs, out_shape = [], []
    for edge, count in zip(edges, counts):
        for kind in (jnp.float32, jnp.bfloat16):
            out_specs.append(part(edge, count))
            out_shape.append(jax.ShapeDtypeStruct((2, tokens, count * width), kind))
    return pl.pallas_call(
        body,
        grid=(steps,),
        in_specs=[
            pl.BlockSpec((2, tokens, feats), lambda j: (0, 0, 0)),
            pl.BlockSpec((feats, width), lambda j: (0, first + j)),
            pl.BlockSpec((width, feats), lambda j: (first + j, 0)),
            pl.BlockSpec((feats // BLOCK, width), lambda j: (0, first + j)),
            pl.BlockSpec((1, blocks, feats), lambda j: (first + j, 0, 0)),
        ],
        out_specs=out_specs,
        out_shape=out_shape,
        compiler_params=PARAMS,
        cost_estimate=pl.CostEstimate(
            flops=4 * tokens * feats * width * steps,
            bytes_accessed=4 * feats * width * steps + 4 * tokens * feats,
            transcendentals=0,
        ),
        name="forward",
    )(pair, up, down, mu, md)


def finish(v, g):
    square = v * v
    t = jnp.tanh(v * (ROOT + (ROOT * CUBE) * square))
    half = 0.5 + 0.5 * t
    slope = half + (0.5 * v) * ((1.0 - t) * (1.0 + t)) * (ROOT + (3.0 * ROOT * CUBE) * square)
    return v * half, g * slope


def chunk_kernel(own, came, up, mu, state, grads, weights, first, count, width):
    _, tokens, chunk = own.shape
    feats, units = up.shape
    blocks = width // BLOCK
    rows = tokens // 2
    n_came = len(came)

    def body(*refs):
        refs = list(refs)
        own_ref = refs.pop(0)
        came_refs = [refs.pop(0) for _ in range(n_came)]
        up_ref, mu_ref = refs.pop(0), refs.pop(0)
        lo_in, hi_in = (refs.pop(0), refs.pop(0)) if state else (None, None)
        if weights:
            tokt_ref, cot_ref, md_ref = refs[:3]
        lo_ref, hi_ref, one_ref, two_ref = refs[-4:]

        @pl.when(pl.program_id(0) == 0)
        def _():
            lo_ref[...] = lo_in[...] if state else jnp.zeros_like(lo_ref)
            hi_ref[...] = hi_in[...] if state else jnp.zeros_like(hi_ref)

        def total(k):
            value = own_ref[k]
            for ref in came_refs:
                value += ref[k].astype(jnp.float32)
            return value

        act, grad = finish(total(0), total(1))
        hgrad = grad.astype(jnp.bfloat16)
        if weights:
            act_t = act.T.astype(jnp.bfloat16)
        else:
            one_ref[...] = act.astype(jnp.bfloat16)
            two_ref[...] = hgrad
        band = min(feats, BAND * BLOCK)
        for b in range(feats // band):
            cut = slice(b * band, (b + 1) * band)
            at = b * (band // BLOCK)
            part = dot(hgrad, masked(up_ref[cut, :], mu_ref, at), ((1,), (1,)))
            lo_ref[:, cut] += part[:rows]
            hi_ref[:, cut] += part[rows:]
            if weights:
                one_ref[cut, :] = masked(dot(tokt_ref[cut, :], hgrad).astype(jnp.bfloat16), mu_ref, at)
                two_ref[:, cut] = masked(dot(act_t, cot_ref[0, :, cut]).astype(jnp.bfloat16), md_ref.at[0], 0, cut)

    part = pl.BlockSpec((2, tokens, width), lambda j: (0, 0, j))
    half_spec = pl.BlockSpec((rows, feats), lambda j: (0, 0))
    half_shape = jax.ShapeDtypeStruct((rows, feats), jnp.float32)
    in_specs = [
        *([part] * (1 + n_came)),
        pl.BlockSpec((feats, width), lambda j: (0, first + j)),
        pl.BlockSpec((feats // BLOCK, width), lambda j: (0, first + j)),
        *([half_spec] * (2 if state else 0)),
    ]
    operands = [own, *came, up, mu, *(state or ())]
    aliases = {}
    if weights:
        in_specs += weight_in_specs(tokens, feats, blocks, first)
        operands += weights
        if grads:
            aliases = {len(operands): 2, len(operands) + 1: 3}
            in_specs += [pl.BlockSpec(memory_space=pl.ANY)] * 2
            operands += grads
        out_specs, out_shape = weight_outs(feats, units, first, width)
    else:
        out_specs = [pl.BlockSpec((tokens, width), lambda j: (0, j))] * 2
        out_shape = [jax.ShapeDtypeStruct((tokens, chunk), jnp.bfloat16)] * 2
    times = 3 if weights else 1
    return pl.pallas_call(
        body,
        grid=(count,),
        in_specs=in_specs,
        out_specs=[half_spec, half_spec, *out_specs],
        out_shape=[half_shape, half_shape, *out_shape],
        input_output_aliases=aliases,
        compiler_params=PARAMS,
        cost_estimate=pl.CostEstimate(
            flops=2 * times * tokens * feats * chunk,
            bytes_accessed=2 * times * feats * chunk + 8 * tokens * feats,
            transcendentals=tokens * chunk,
        ),
        name="chunk",
    )(*operands)


def transposed(pair):
    _, tokens, feats = pair.shape

    def body(pair_ref, out_ref):
        out_ref[...] = pair_ref[0].astype(jnp.float32).T.astype(out_ref.dtype)

    return pl.pallas_call(
        body,
        grid=(1,),
        in_specs=[pl.BlockSpec((1, tokens, feats), lambda j: (0, 0, 0))],
        out_specs=pl.BlockSpec((feats, tokens), lambda j: (0, 0)),
        out_shape=jax.ShapeDtypeStruct((feats, tokens), pair.dtype),
        compiler_params=PARAMS,
        cost_estimate=pl.CostEstimate(flops=0, bytes_accessed=4 * tokens * feats, transcendentals=0),
        name="transposed",
    )(pair)


def weight_in_specs(tokens, feats, blocks, first):
    return [
        pl.BlockSpec((feats, tokens), lambda j: (0, 0)),
        pl.BlockSpec((1, tokens, feats), lambda j: (1, 0, 0)),
        pl.BlockSpec((1, blocks, feats), lambda j: (first + j, 0, 0)),
    ]


def weight_outs(feats, units, first, width):
    specs = [
        pl.BlockSpec((feats, width), lambda j: (0, first + j)),
        pl.BlockSpec((width, feats), lambda j: (first + j, 0)),
    ]
    return specs, [pltpu.HBM((feats, units), jnp.bfloat16), pltpu.HBM((units, feats), jnp.bfloat16)]


def weight_grads(act, hgrad, mu, weights, grads, units, first, count, width):
    tokens, feats = weights[1].shape[1:]

    def body(tokt_ref, cot_ref, md_ref, act_ref, hgrad_ref, mu_ref, *refs):
        upg_ref, dng_ref = refs[-2:]
        hgrad = hgrad_ref[...]
        act_t = act_ref[...].astype(jnp.float32).T.astype(jnp.bfloat16)
        band = min(feats, BAND * BLOCK)
        for b in range(feats // band):
            cut = slice(b * band, (b + 1) * band)
            upg_ref[cut, :] = masked(dot(tokt_ref[cut, :], hgrad).astype(jnp.bfloat16), mu_ref, b * (band // BLOCK))
            dng_ref[:, cut] = masked(dot(act_t, cot_ref[0, :, cut]).astype(jnp.bfloat16), md_ref.at[0], 0, cut)

    part = pl.BlockSpec((tokens, width), lambda j: (0, j))
    any_spec = pl.BlockSpec(memory_space=pl.ANY)
    out_specs, out_shape = weight_outs(feats, units, first, width)
    return pl.pallas_call(
        body,
        grid=(count,),
        in_specs=[
            *weight_in_specs(tokens, feats, width // BLOCK, first),
            part,
            part,
            pl.BlockSpec((feats // BLOCK, width), lambda j: (0, first + j)),
            *([any_spec] * (2 if grads else 0)),
        ],
        out_specs=out_specs,
        out_shape=out_shape,
        input_output_aliases={6: 0, 7: 1} if grads else {},
        compiler_params=PARAMS,
        cost_estimate=pl.CostEstimate(
            flops=4 * tokens * feats * width * count,
            bytes_accessed=4 * feats * width * count + 4 * tokens * feats,
            transcendentals=0,
        ),
        name="weight_grads",
    )(*weights, act, hgrad, mu, *(grads or ()))


def xor_pairs(n, bits):
    return [(i, i ^ bits) for i in range(n)]


def gather_tokens(x, n, masks):
    if n == 1:
        return x, masks
    parts = [x] + [lax.ppermute(x, "col", xor_pairs(n, s)) for s in range(2, n, 2)]
    half = jnp.concatenate(parts, axis=1)
    half, masks = lax.optimization_barrier((half, masks))
    return jnp.concatenate([half, lax.ppermute(half, "col", xor_pairs(n, 1))], axis=1), masks


def scatter_tokens(lo, hi, n):
    mine = lo + lax.ppermute(hi, "col", xor_pairs(n, 1))
    rows = 2 * mine.shape[0] // n
    send = mine[rows:].astype(jnp.bfloat16)
    out = mine[:rows]
    for k, s in enumerate(range(2, n, 2)):
        came = lax.ppermute(send[k * rows:(k + 1) * rows], "col", xor_pairs(n, s))
        out = out + came.astype(jnp.float32)
    return out


def shift(x, pairs):
    return lax.ppermute(x, "row", pairs)


def local(rows, cols, tokens, cotangent, up_weight, down_weight, block_index):
    feats, units = up_weight.shape
    row_blocks = feats // BLOCK
    col_blocks = units // BLOCK
    hits = tile_mask(block_index, row_blocks, col_blocks).astype(jnp.float32)
    width = PAIR * BLOCK
    mu = jnp.repeat(hits, BLOCK, axis=1)
    md = jnp.repeat(hits.T, BLOCK, axis=1).reshape(units // width, PAIR, feats)
    pair, (mu, md) = gather_tokens(jnp.stack([tokens, cotangent]), cols, (mu, md))
    up_weight, down_weight = (pltpu.with_memory_space_constraint(w, pltpu.HBM) for w in (up_weight, down_weight))
    tokt = transposed(pair)
    weights = [tokt, pair, md]
    plan = chunk_steps(units // width)
    owns = []
    while len(owns) < len(plan):
        group = plan[len(owns):len(owns) + GROUPS[min(len(owns), len(GROUPS) - 1)]]
        outs = forward(pair, up_weight, down_weight, mu, md, group[0][0], [n for _, n in group], width)
        owns += list(zip(outs[::2], outs[1::2]))
    right = rows // 2
    sums = []
    for own, near in owns:
        came = []
        for k in range(right - 1):
            came.append(shift(near, [(k, k + 1), (rows - 1 - k, rows - 2 - k)]))
            near = (own + sum(x.astype(jnp.float32) for x in came)).astype(jnp.bfloat16)
        came.append(shift(near, [(right - 1, right), (right, right - 1)]))
        out = own + came[-1].astype(jnp.float32)
        for k in reversed(range(right - 1)):
            far = shift(out.astype(jnp.bfloat16), [(k + 1, k), (rows - 2 - k, rows - 1 - k)])
            came.append(far)
            out = out + far.astype(jnp.float32)
        sums.append((own, came))
    state = grads = None
    late = []
    for c, (first, count) in enumerate(plan):
        whole_chunk = c + LATE < len(plan)
        *state, one, two = chunk_kernel(
            *sums[c], up_weight, mu, state, grads, weights if whole_chunk else None, first, count, width
        )
        if whole_chunk:
            grads = [one, two]
        else:
            late.append((c, first, count, one, two))
    for c, first, count, act, hgrad in late:
        grads = weight_grads(act, hgrad, mu, weights, grads, units, first, count, width)
    input_grad = scatter_tokens(*state, cols)
    return (input_grad.astype(jnp.bfloat16), *grads)


def whole(rows, cols, *arrays):
    return local(rows, cols, *arrays)


def solution(mesh):
    return jax.shard_map(
        functools.partial(whole, mesh.shape["row"], mesh.shape["col"]),
        mesh=mesh,
        in_specs=(P("col", "row"), P("col", "row"), P("row", "col"), P("col", "row"), P()),
        out_specs=(P("col", "row"), P("row", "col"), P("col", "row")),
        check_vma=False,
    )
```

```python
import functools

import jax
import jax.numpy as jnp
from jax import lax
from jax.experimental import pallas as pl
from jax.experimental.pallas import tpu as pltpu
from jax.sharding import PartitionSpec as P


BLOCK = 128
SUB = 16
PAIR = 2
VMEM_LIMIT = 20 * 1024 * 1024
PARAMS = pltpu.CompilerParams(vmem_limit_bytes=VMEM_LIMIT)
SHARES = (2, 4, 4, 4, 2)
GROUPS = (1, 1, 1, 1, 1)
LATE = 1
BAND = 4
MERGED = ()
ROOT = 0.7978845608028654
CUBE = 0.044715


def chunk_steps(steps):
    total = sum(SHARES)
    edges = [0]
    run = 0
    for share in SHARES:
        run += share
        edge = (run * steps) // total
        if edge > edges[-1]:
            edges.append(edge)
    return [(a, b - a) for a, b in zip(edges[:-1], edges[1:])]


def tile_mask(block_index, row_blocks, col_blocks):
    row_place = lax.axis_index("row")
    col_place = lax.axis_index("col")
    own_rows = lax.dynamic_slice_in_dim(block_index, row_place * row_blocks, row_blocks, 0)
    own_cols = col_place * col_blocks + jnp.arange(col_blocks, dtype=jnp.int32)
    return jnp.any(own_rows[:, :, None] == own_cols[None, None, :], axis=1)


def masked(block, mask_ref, first, cut=slice(None)):
    rows, width = block.shape
    parts = []
    for g in range(rows // BLOCK):
        row = jnp.broadcast_to(mask_ref[first + g:first + g + 1, cut], (SUB, width)).astype(block.dtype)
        part = block[g * BLOCK:(g + 1) * BLOCK].reshape(BLOCK // SUB, SUB, width) * row[None]
        parts.append(part.reshape(BLOCK, width))
    return jnp.concatenate(parts, axis=0) if len(parts) > 1 else parts[0]


def dot(a, b, dims=((1,), (0,))):
    return lax.dot_general(a, b, (dims, ((), ())), preferred_element_type=jnp.float32)


def forward(pair, up, down, mu, md, first, counts, width):
    _, tokens, feats = pair.shape
    blocks = width // BLOCK
    steps = sum(counts)
    edges = [sum(counts[:k]) for k in range(len(counts))]

    def body(pair_ref, up_ref, down_ref, mu_ref, md_ref, *out_refs):
        step = pl.program_id(0)
        hidden = dot(pair_ref[0], masked(up_ref[...], mu_ref, 0))
        grad = dot(pair_ref[1], masked(down_ref[...], md_ref.at[0], 0), ((1,), (1,)))
        for k, (edge, count) in enumerate(zip(edges, counts)):
            def put(k=k):
                own_ref, send_ref = out_refs[2 * k:2 * k + 2]
                own_ref[0] = hidden
                own_ref[1] = grad
                send_ref[0] = hidden.astype(send_ref.dtype)
                send_ref[1] = grad.astype(send_ref.dtype)

            if len(counts) == 1:
                put()
            else:
                pl.when((step >= edge) & (step < edge + count))(put)

    def part(edge, count):
        return pl.BlockSpec((2, tokens, width), lambda j: (0, 0, jnp.clip(j - edge, 0, count - 1)))

    out_specs, out_shape = [], []
    for edge, count in zip(edges, counts):
        for kind in (jnp.float32, jnp.bfloat16):
            out_specs.append(part(edge, count))
            out_shape.append(jax.ShapeDtypeStruct((2, tokens, count * width), kind))
    return pl.pallas_call(
        body,
        grid=(steps,),
        in_specs=[
            pl.BlockSpec((2, tokens, feats), lambda j: (0, 0, 0)),
            pl.BlockSpec((feats, width), lambda j: (0, first + j)),
            pl.BlockSpec((width, feats), lambda j: (first + j, 0)),
            pl.BlockSpec((feats // BLOCK, width), lambda j: (0, first + j)),
            pl.BlockSpec((1, blocks, feats), lambda j: (first + j, 0, 0)),
        ],
        out_specs=out_specs,
        out_shape=out_shape,
        compiler_params=PARAMS,
        cost_estimate=pl.CostEstimate(
            flops=4 * tokens * feats * width * steps,
            bytes_accessed=4 * feats * width * steps + 4 * tokens * feats,
            transcendentals=0,
        ),
        name="forward",
    )(pair, up, down, mu, md)


def finish(v, g):
    square = v * v
    t = jnp.tanh(v * (ROOT + (ROOT * CUBE) * square))
    half = 0.5 + 0.5 * t
    slope = half + (0.5 * v) * ((1.0 - t) * (1.0 + t)) * (ROOT + (3.0 * ROOT * CUBE) * square)
    return v * half, g * slope


def chunk_kernel(own, came, flags, up, mu, state, grads, weights, first, count, width):
    _, tokens, chunk = own.shape
    feats, units = up.shape
    blocks = width // BLOCK
    rows = tokens // 2
    n_came = len(came)

    def body(*refs):
        refs = list(refs)
        flag_ref, own_ref = refs.pop(0), refs.pop(0)
        came_refs = [refs.pop(0) for _ in range(n_came)]
        up_ref, mu_ref = refs.pop(0), refs.pop(0)
        lo_in, hi_in = (refs.pop(0), refs.pop(0)) if state else (None, None)
        if weights:
            tokt_ref, cot_ref, md_ref = refs[:3]
        lo_ref, hi_ref, one_ref, two_ref = refs[-4:]

        @pl.when(pl.program_id(0) == 0)
        def _():
            lo_ref[...] = lo_in[...] if state else jnp.zeros_like(lo_ref)
            hi_ref[...] = hi_in[...] if state else jnp.zeros_like(hi_ref)

        def total(k):
            value = own_ref[k]
            for ref, (_, flag) in zip(came_refs, came):
                part = ref[k].astype(jnp.float32)
                value += part if flag is None else part * flag_ref[flag]
            return value

        act, grad = finish(total(0), total(1))
        hgrad = grad.astype(jnp.bfloat16)
        if weights:
            act_t = act.T.astype(jnp.bfloat16)
        else:
            one_ref[...] = act.astype(jnp.bfloat16)
            two_ref[...] = hgrad
        band = min(feats, BAND * BLOCK)
        for b in range(feats // band):
            cut = slice(b * band, (b + 1) * band)
            at = b * (band // BLOCK)
            part = dot(hgrad, masked(up_ref[cut, :], mu_ref, at), ((1,), (1,)))
            lo_ref[:, cut] += part[:rows]
            hi_ref[:, cut] += part[rows:]
            if weights:
                one_ref[cut, :] = masked(dot(tokt_ref[cut, :], hgrad).astype(jnp.bfloat16), mu_ref, at)
                two_ref[:, cut] = masked(dot(act_t, cot_ref[0, :, cut]).astype(jnp.bfloat16), md_ref.at[0], 0, cut)

    part = pl.BlockSpec((2, tokens, width), lambda j: (0, 0, j))
    half_spec = pl.BlockSpec((rows, feats), lambda j: (0, 0))
    half_shape = jax.ShapeDtypeStruct((rows, feats), jnp.float32)
    in_specs = [
        pl.BlockSpec(memory_space=pltpu.SMEM),
        *([part] * (1 + n_came)),
        pl.BlockSpec((feats, width), lambda j: (0, first + j)),
        pl.BlockSpec((feats // BLOCK, width), lambda j: (0, first + j)),
        *([half_spec] * (2 if state else 0)),
    ]
    operands = [flags, own, *(x for x, _ in came), up, mu, *(state or ())]
    aliases = {}
    if weights:
        in_specs += weight_in_specs(tokens, feats, blocks, first)
        operands += weights
        if grads:
            aliases = {len(operands): 2, len(operands) + 1: 3}
            in_specs += [pl.BlockSpec(memory_space=pl.ANY)] * 2
            operands += grads
        out_specs, out_shape = weight_outs(feats, units, first, width)
    else:
        out_specs = [pl.BlockSpec((tokens, width), lambda j: (0, j))] * 2
        out_shape = [jax.ShapeDtypeStruct((tokens, chunk), jnp.bfloat16)] * 2
    times = 3 if weights else 1
    return pl.pallas_call(
        body,
        grid=(count,),
        in_specs=in_specs,
        out_specs=[half_spec, half_spec, *out_specs],
        out_shape=[half_shape, half_shape, *out_shape],
        input_output_aliases=aliases,
        compiler_params=PARAMS,
        cost_estimate=pl.CostEstimate(
            flops=2 * times * tokens * feats * chunk,
            bytes_accessed=2 * times * feats * chunk + 8 * tokens * feats,
            transcendentals=tokens * chunk,
        ),
        name="chunk",
    )(*operands)


def transposed(pair):
    _, tokens, feats = pair.shape

    def body(pair_ref, out_ref):
        out_ref[...] = pair_ref[0].astype(jnp.float32).T.astype(out_ref.dtype)

    return pl.pallas_call(
        body,
        grid=(1,),
        in_specs=[pl.BlockSpec((1, tokens, feats), lambda j: (0, 0, 0))],
        out_specs=pl.BlockSpec((feats, tokens), lambda j: (0, 0)),
        out_shape=jax.ShapeDtypeStruct((feats, tokens), pair.dtype),
        compiler_params=PARAMS,
        cost_estimate=pl.CostEstimate(flops=0, bytes_accessed=4 * tokens * feats, transcendentals=0),
        name="transposed",
    )(pair)


def weight_in_specs(tokens, feats, blocks, first):
    return [
        pl.BlockSpec((feats, tokens), lambda j: (0, 0)),
        pl.BlockSpec((1, tokens, feats), lambda j: (1, 0, 0)),
        pl.BlockSpec((1, blocks, feats), lambda j: (first + j, 0, 0)),
    ]


def weight_outs(feats, units, first, width):
    specs = [
        pl.BlockSpec((feats, width), lambda j: (0, first + j)),
        pl.BlockSpec((width, feats), lambda j: (first + j, 0)),
    ]
    return specs, [pltpu.HBM((feats, units), jnp.bfloat16), pltpu.HBM((units, feats), jnp.bfloat16)]


def weight_grads(act, hgrad, mu, weights, grads, units, first, count, width):
    tokens, feats = weights[1].shape[1:]

    def body(tokt_ref, cot_ref, md_ref, act_ref, hgrad_ref, mu_ref, *refs):
        upg_ref, dng_ref = refs[-2:]
        hgrad = hgrad_ref[...]
        act_t = act_ref[...].astype(jnp.float32).T.astype(jnp.bfloat16)
        band = min(feats, BAND * BLOCK)
        for b in range(feats // band):
            cut = slice(b * band, (b + 1) * band)
            upg_ref[cut, :] = masked(dot(tokt_ref[cut, :], hgrad).astype(jnp.bfloat16), mu_ref, b * (band // BLOCK))
            dng_ref[:, cut] = masked(dot(act_t, cot_ref[0, :, cut]).astype(jnp.bfloat16), md_ref.at[0], 0, cut)

    part = pl.BlockSpec((tokens, width), lambda j: (0, j))
    any_spec = pl.BlockSpec(memory_space=pl.ANY)
    out_specs, out_shape = weight_outs(feats, units, first, width)
    return pl.pallas_call(
        body,
        grid=(count,),
        in_specs=[
            *weight_in_specs(tokens, feats, width // BLOCK, first),
            part,
            part,
            pl.BlockSpec((feats // BLOCK, width), lambda j: (0, first + j)),
            *([any_spec] * (2 if grads else 0)),
        ],
        out_specs=out_specs,
        out_shape=out_shape,
        input_output_aliases={6: 0, 7: 1} if grads else {},
        compiler_params=PARAMS,
        cost_estimate=pl.CostEstimate(
            flops=4 * tokens * feats * width * count,
            bytes_accessed=4 * feats * width * count + 4 * tokens * feats,
            transcendentals=0,
        ),
        name="weight_grads",
    )(*weights, act, hgrad, mu, *(grads or ()))


def xor_pairs(n, bits):
    return [(i, i ^ bits) for i in range(n)]


def gather_tokens(x, n, masks):
    if n == 1:
        return x, masks
    parts = [x] + [lax.ppermute(x, "col", xor_pairs(n, s)) for s in range(2, n, 2)]
    half = jnp.concatenate(parts, axis=1)
    half, masks = lax.optimization_barrier((half, masks))
    return jnp.concatenate([half, lax.ppermute(half, "col", xor_pairs(n, 1))], axis=1), masks


def scatter_tokens(lo, hi, n):
    mine = lo + lax.ppermute(hi, "col", xor_pairs(n, 1))
    rows = 2 * mine.shape[0] // n
    send = mine[rows:].astype(jnp.bfloat16)
    out = mine[:rows]
    for k, s in enumerate(range(2, n, 2)):
        came = lax.ppermute(send[k * rows:(k + 1) * rows], "col", xor_pairs(n, s))
        out = out + came.astype(jnp.float32)
    return out


def shift(x, pairs):
    return lax.ppermute(x, "row", pairs)


def local(rows, cols, tokens, cotangent, up_weight, down_weight, block_index):
    feats, units = up_weight.shape
    row_blocks = feats // BLOCK
    col_blocks = units // BLOCK
    hits = tile_mask(block_index, row_blocks, col_blocks).astype(jnp.float32)
    width = PAIR * BLOCK
    mu = jnp.repeat(hits, BLOCK, axis=1)
    md = jnp.repeat(hits.T, BLOCK, axis=1).reshape(units // width, PAIR, feats)
    pair, (mu, md) = gather_tokens(jnp.stack([tokens, cotangent]), cols, (mu, md))
    up_weight, down_weight = (pltpu.with_memory_space_constraint(w, pltpu.HBM) for w in (up_weight, down_weight))
    tokt = transposed(pair)
    weights = [tokt, pair, md]
    plan = chunk_steps(units // width)
    owns = []
    while len(owns) < len(plan):
        group = plan[len(owns):len(owns) + GROUPS[min(len(owns), len(GROUPS) - 1)]]
        outs = forward(pair, up_weight, down_weight, mu, md, group[0][0], [n for _, n in group], width)
        owns += list(zip(outs[::2], outs[1::2]))
    right = rows // 2
    place = lax.axis_index("row")
    is_outer = (place == 0) | (place == rows - 1)
    flags = jnp.stack([~is_outer, is_outer]).astype(jnp.float32)
    joined = dict(MERGED) if right == 2 else {}
    joined = {f: k for f, k in joined.items() if f < len(plan) and plan[f][1] == plan[k][1]}
    came = [[] for _ in plan]
    outs = []
    for c, (own, near) in enumerate(owns):
        if c in joined:
            other = joined[c]
            send = jnp.where(is_outer, near, outs[other].astype(jnp.bfloat16))
            x = shift(send, [(0, 1), (1, 0), (2, 3), (3, 2)])
            came[c].append((x, 0))
            came[other].append((x, 1))
            near = (own + jnp.where(is_outer, 0.0, x.astype(jnp.float32))).astype(jnp.bfloat16)
        else:
            for k in range(right - 1):
                came[c].append((shift(near, [(k, k + 1), (rows - 1 - k, rows - 2 - k)]), None))
                near = (own + sum(x.astype(jnp.float32) for x, _ in came[c])).astype(jnp.bfloat16)
        mid = shift(near, [(right - 1, right), (right, right - 1)])
        came[c].append((mid, None))
        outs.append(own + mid.astype(jnp.float32))
    for c, out in enumerate(outs):
        if c in joined.values():
            continue
        for k in reversed(range(right - 1)):
            send = out.astype(jnp.bfloat16)
            far = shift(send, [(k + 1, k), (rows - 2 - k, rows - 1 - k)])
            came[c].append((far, None))
            out = out + far.astype(jnp.float32)
    sums = [(own, part) for (own, _), part in zip(owns, came)]
    state = grads = None
    late = []
    for c, (first, count) in enumerate(plan):
        whole_chunk = c + LATE < len(plan)
        *state, one, two = chunk_kernel(
            *sums[c], flags, up_weight, mu, state, grads, weights if whole_chunk else None, first, count, width
        )
        if whole_chunk:
            grads = [one, two]
        else:
            late.append((c, first, count, one, two))
    for c, first, count, act, hgrad in late:
        grads = weight_grads(act, hgrad, mu, weights, grads, units, first, count, width)
    input_grad = scatter_tokens(*state, cols)
    return (input_grad.astype(jnp.bfloat16), *grads)


def whole(rows, cols, *arrays):
    return local(rows, cols, *arrays)


def solution(mesh):
    return jax.shard_map(
        functools.partial(whole, mesh.shape["row"], mesh.shape["col"]),
        mesh=mesh,
        in_specs=(P("col", "row"), P("col", "row"), P("row", "col"), P("col", "row"), P()),
        out_specs=(P("col", "row"), P("row", "col"), P("col", "row")),
        check_vma=False,
    )
```

```python
import functools

import jax
import jax.numpy as jnp
from jax import lax
from jax.experimental import pallas as pl
from jax.experimental.pallas import tpu as pltpu
from jax.sharding import PartitionSpec as P


BLOCK = 128
SUB = 16
PAIR = 2
VMEM_LIMIT = 20 * 1024 * 1024
PARAMS = pltpu.CompilerParams(vmem_limit_bytes=VMEM_LIMIT)
SHARES = (2, 4, 4, 4, 2)
GROUPS = (1, 1, 1, 1, 1)
LATE = 1
BAND = 4
MERGED = ()
ROOT = 0.7978845608028654
CUBE = 0.044715


def chunk_steps(steps):
    total = sum(SHARES)
    edges = [0]
    run = 0
    for share in SHARES:
        run += share
        edge = (run * steps) // total
        if edge > edges[-1]:
            edges.append(edge)
    return [(a, b - a) for a, b in zip(edges[:-1], edges[1:])]


def tile_mask(block_index, row_blocks, col_blocks):
    row_place = lax.axis_index("row")
    col_place = lax.axis_index("col")
    own_rows = lax.dynamic_slice_in_dim(block_index, row_place * row_blocks, row_blocks, 0)
    own_cols = col_place * col_blocks + jnp.arange(col_blocks, dtype=jnp.int32)
    return jnp.any(own_rows[:, :, None] == own_cols[None, None, :], axis=1)


def masked(block, mask_ref, first, cut=slice(None)):
    rows, width = block.shape
    parts = []
    for g in range(rows // BLOCK):
        row = jnp.broadcast_to(mask_ref[first + g:first + g + 1, cut], (SUB, width)).astype(block.dtype)
        part = block[g * BLOCK:(g + 1) * BLOCK].reshape(BLOCK // SUB, SUB, width) * row[None]
        parts.append(part.reshape(BLOCK, width))
    return jnp.concatenate(parts, axis=0) if len(parts) > 1 else parts[0]


def dot(a, b, dims=((1,), (0,))):
    return lax.dot_general(a, b, (dims, ((), ())), preferred_element_type=jnp.float32)


def forward(pair, up, down, mu, md, first, counts, width):
    _, tokens, feats = pair.shape
    blocks = width // BLOCK
    steps = sum(counts)
    edges = [sum(counts[:k]) for k in range(len(counts))]

    def body(pair_ref, up_ref, down_ref, mu_ref, md_ref, *out_refs):
        step = pl.program_id(0)
        hidden = dot(pair_ref[0], masked(up_ref[...], mu_ref, 0))
        grad = dot(pair_ref[1], masked(down_ref[...], md_ref.at[0], 0), ((1,), (1,)))
        for k, (edge, count) in enumerate(zip(edges, counts)):
            def put(k=k):
                own_ref, send_ref = out_refs[2 * k:2 * k + 2]
                own_ref[0] = hidden
                own_ref[1] = grad
                send_ref[0] = hidden.astype(send_ref.dtype)
                send_ref[1] = grad.astype(send_ref.dtype)

            if len(counts) == 1:
                put()
            else:
                pl.when((step >= edge) & (step < edge + count))(put)

    def part(edge, count):
        return pl.BlockSpec((2, tokens, width), lambda j: (0, 0, jnp.clip(j - edge, 0, count - 1)))

    out_specs, out_shape = [], []
    for edge, count in zip(edges, counts):
        for kind in (jnp.float32, jnp.bfloat16):
            out_specs.append(part(edge, count))
            out_shape.append(jax.ShapeDtypeStruct((2, tokens, count * width), kind))
    return pl.pallas_call(
        body,
        grid=(steps,),
        in_specs=[
            pl.BlockSpec((2, tokens, feats), lambda j: (0, 0, 0)),
            pl.BlockSpec((feats, width), lambda j: (0, first + j)),
            pl.BlockSpec((width, feats), lambda j: (first + j, 0)),
            pl.BlockSpec((feats // BLOCK, width), lambda j: (0, first + j)),
            pl.BlockSpec((1, blocks, feats), lambda j: (first + j, 0, 0)),
        ],
        out_specs=out_specs,
        out_shape=out_shape,
        compiler_params=PARAMS,
        cost_estimate=pl.CostEstimate(
            flops=4 * tokens * feats * width * steps,
            bytes_accessed=4 * feats * width * steps + 4 * tokens * feats,
            transcendentals=0,
        ),
        name="forward",
    )(pair, up, down, mu, md)


def finish(v, g):
    square = v * v
    t = jnp.tanh(v * (ROOT + (ROOT * CUBE) * square))
    half = 0.5 + 0.5 * t
    slope = half + (0.5 * v) * ((1.0 - t) * (1.0 + t)) * (ROOT + (3.0 * ROOT * CUBE) * square)
    return v * half, g * slope


def chunk_kernel(own, came, flags, up, mu, state, grads, weights, first, count, width):
    _, tokens, chunk = own.shape
    feats, units = up.shape
    blocks = width // BLOCK
    rows = tokens // 2
    n_came = len(came)

    def body(*refs):
        refs = list(refs)
        flag_ref, own_ref = refs.pop(0), refs.pop(0)
        came_refs = [refs.pop(0) for _ in range(n_came)]
        up_ref, mu_ref = refs.pop(0), refs.pop(0)
        lo_in, hi_in = (refs.pop(0), refs.pop(0)) if state else (None, None)
        if weights:
            tokt_ref, cot_ref, md_ref = refs[:3]
        lo_ref, hi_ref, one_ref, two_ref = refs[-4:]

        @pl.when(pl.program_id(0) == 0)
        def _():
            lo_ref[...] = lo_in[...] if state else jnp.zeros_like(lo_ref)
            hi_ref[...] = hi_in[...] if state else jnp.zeros_like(hi_ref)

        def total(k):
            value = own_ref[k]
            for ref, (_, flag) in zip(came_refs, came):
                part = ref[k].astype(jnp.float32)
                value += part if flag is None else part * flag_ref[flag]
            return value

        act, grad = finish(total(0), total(1))
        hgrad = grad.astype(jnp.bfloat16)
        if weights:
            act_t = act.T.astype(jnp.bfloat16)
        else:
            one_ref[...] = act.astype(jnp.bfloat16)
            two_ref[...] = hgrad
        band = min(feats, BAND * BLOCK)
        for b in range(feats // band):
            cut = slice(b * band, (b + 1) * band)
            at = b * (band // BLOCK)
            part = dot(hgrad, masked(up_ref[cut, :], mu_ref, at), ((1,), (1,)))
            lo_ref[:, cut] += part[:rows]
            hi_ref[:, cut] += part[rows:]
            if weights:
                one_ref[cut, :] = masked(dot(tokt_ref[cut, :], hgrad).astype(jnp.bfloat16), mu_ref, at)
                two_ref[:, cut] = masked(dot(act_t, cot_ref[0, :, cut]).astype(jnp.bfloat16), md_ref.at[0], 0, cut)

    part = pl.BlockSpec((2, tokens, width), lambda j: (0, 0, j))
    half_spec = pl.BlockSpec((rows, feats), lambda j: (0, 0))
    half_shape = jax.ShapeDtypeStruct((rows, feats), jnp.float32)
    in_specs = [
        pl.BlockSpec(memory_space=pltpu.SMEM),
        *([part] * (1 + n_came)),
        pl.BlockSpec((feats, width), lambda j: (0, first + j)),
        pl.BlockSpec((feats // BLOCK, width), lambda j: (0, first + j)),
        *([half_spec] * (2 if state else 0)),
    ]
    operands = [flags, own, *(x for x, _ in came), up, mu, *(state or ())]
    aliases = {}
    if weights:
        in_specs += weight_in_specs(tokens, feats, blocks, first)
        operands += weights
        if grads:
            aliases = {len(operands): 2, len(operands) + 1: 3}
            in_specs += [pl.BlockSpec(memory_space=pl.ANY)] * 2
            operands += grads
        out_specs, out_shape = weight_outs(feats, units, first, width)
    else:
        out_specs = [pl.BlockSpec((tokens, width), lambda j: (0, j))] * 2
        out_shape = [jax.ShapeDtypeStruct((tokens, chunk), jnp.bfloat16)] * 2
    times = 3 if weights else 1
    return pl.pallas_call(
        body,
        grid=(count,),
        in_specs=in_specs,
        out_specs=[half_spec, half_spec, *out_specs],
        out_shape=[half_shape, half_shape, *out_shape],
        input_output_aliases=aliases,
        compiler_params=PARAMS,
        cost_estimate=pl.CostEstimate(
            flops=2 * times * tokens * feats * chunk,
            bytes_accessed=2 * times * feats * chunk + 8 * tokens * feats,
            transcendentals=tokens * chunk,
        ),
        name="chunk",
    )(*operands)


def transposed(pair):
    _, tokens, feats = pair.shape

    def body(pair_ref, out_ref):
        out_ref[...] = pair_ref[0].astype(jnp.float32).T.astype(out_ref.dtype)

    return pl.pallas_call(
        body,
        grid=(1,),
        in_specs=[pl.BlockSpec((1, tokens, feats), lambda j: (0, 0, 0))],
        out_specs=pl.BlockSpec((feats, tokens), lambda j: (0, 0)),
        out_shape=jax.ShapeDtypeStruct((feats, tokens), pair.dtype),
        compiler_params=PARAMS,
        cost_estimate=pl.CostEstimate(flops=0, bytes_accessed=4 * tokens * feats, transcendentals=0),
        name="transposed",
    )(pair)


def weight_in_specs(tokens, feats, blocks, first):
    return [
        pl.BlockSpec((feats, tokens), lambda j: (0, 0)),
        pl.BlockSpec((1, tokens, feats), lambda j: (1, 0, 0)),
        pl.BlockSpec((1, blocks, feats), lambda j: (first + j, 0, 0)),
    ]


def weight_outs(feats, units, first, width):
    specs = [
        pl.BlockSpec((feats, width), lambda j: (0, first + j)),
        pl.BlockSpec((width, feats), lambda j: (first + j, 0)),
    ]
    return specs, [pltpu.HBM((feats, units), jnp.bfloat16), pltpu.HBM((units, feats), jnp.bfloat16)]


def weight_grads(act, hgrad, mu, weights, grads, units, first, count, width):
    tokens, feats = weights[1].shape[1:]

    def body(tokt_ref, cot_ref, md_ref, act_ref, hgrad_ref, mu_ref, *refs):
        upg_ref, dng_ref = refs[-2:]
        hgrad = hgrad_ref[...]
        act_t = act_ref[...].astype(jnp.float32).T.astype(jnp.bfloat16)
        band = min(feats, BAND * BLOCK)
        for b in range(feats // band):
            cut = slice(b * band, (b + 1) * band)
            upg_ref[cut, :] = masked(dot(tokt_ref[cut, :], hgrad).astype(jnp.bfloat16), mu_ref, b * (band // BLOCK))
            dng_ref[:, cut] = masked(dot(act_t, cot_ref[0, :, cut]).astype(jnp.bfloat16), md_ref.at[0], 0, cut)

    part = pl.BlockSpec((tokens, width), lambda j: (0, j))
    any_spec = pl.BlockSpec(memory_space=pl.ANY)
    out_specs, out_shape = weight_outs(feats, units, first, width)
    return pl.pallas_call(
        body,
        grid=(count,),
        in_specs=[
            *weight_in_specs(tokens, feats, width // BLOCK, first),
            part,
            part,
            pl.BlockSpec((feats // BLOCK, width), lambda j: (0, first + j)),
            *([any_spec] * (2 if grads else 0)),
        ],
        out_specs=out_specs,
        out_shape=out_shape,
        input_output_aliases={6: 0, 7: 1} if grads else {},
        compiler_params=PARAMS,
        cost_estimate=pl.CostEstimate(
            flops=4 * tokens * feats * width * count,
            bytes_accessed=4 * feats * width * count + 4 * tokens * feats,
            transcendentals=0,
        ),
        name="weight_grads",
    )(*weights, act, hgrad, mu, *(grads or ()))


def xor_pairs(n, bits):
    return [(i, i ^ bits) for i in range(n)]


def join(parts, axis):
    shape = list(parts[0].shape)
    step = shape[axis]
    shape[axis] = step * len(parts)
    out = jnp.zeros(shape, parts[0].dtype)
    for k, part in enumerate(parts):
        out = lax.dynamic_update_slice_in_dim(out, part, k * step, axis)
    return out


def gather_tokens(x, n, masks):
    if n == 1:
        return x, masks
    parts = [x] + [lax.ppermute(x, "col", xor_pairs(n, s)) for s in range(2, n, 2)]
    half = join(parts, 1)
    half, masks = lax.optimization_barrier((half, masks))
    return jnp.concatenate([half, lax.ppermute(half, "col", xor_pairs(n, 1))], axis=1), masks


def scatter_tokens(lo, hi, n):
    mine = lo + lax.ppermute(hi, "col", xor_pairs(n, 1))
    rows = 2 * mine.shape[0] // n
    send = mine[rows:].astype(jnp.bfloat16)
    out = mine[:rows]
    for k, s in enumerate(range(2, n, 2)):
        came = lax.ppermute(send[k * rows:(k + 1) * rows], "col", xor_pairs(n, s))
        out = out + came.astype(jnp.float32)
    return out


def shift(x, pairs):
    return lax.ppermute(x, "row", pairs)


def local(rows, cols, tokens, cotangent, up_weight, down_weight, block_index):
    feats, units = up_weight.shape
    row_blocks = feats // BLOCK
    col_blocks = units // BLOCK
    hits = tile_mask(block_index, row_blocks, col_blocks).astype(jnp.float32)
    width = PAIR * BLOCK
    mu = jnp.repeat(hits, BLOCK, axis=1)
    md = jnp.repeat(hits.T, BLOCK, axis=1).reshape(units // width, PAIR, feats)
    pair, (mu, md) = gather_tokens(jnp.stack([tokens, cotangent]), cols, (mu, md))
    up_weight, down_weight = (pltpu.with_memory_space_constraint(w, pltpu.HBM) for w in (up_weight, down_weight))
    tokt = transposed(pair)
    weights = [tokt, pair, md]
    plan = chunk_steps(units // width)
    owns = []
    while len(owns) < len(plan):
        group = plan[len(owns):len(owns) + GROUPS[min(len(owns), len(GROUPS) - 1)]]
        outs = forward(pair, up_weight, down_weight, mu, md, group[0][0], [n for _, n in group], width)
        owns += list(zip(outs[::2], outs[1::2]))
    right = rows // 2
    place = lax.axis_index("row")
    is_outer = (place == 0) | (place == rows - 1)
    flags = jnp.stack([~is_outer, is_outer]).astype(jnp.float32)
    joined = dict(MERGED) if right == 2 else {}
    joined = {f: k for f, k in joined.items() if f < len(plan) and plan[f][1] == plan[k][1]}
    came = [[] for _ in plan]
    outs = []
    for c, (own, near) in enumerate(owns):
        if c in joined:
            other = joined[c]
            send = jnp.where(is_outer, near, outs[other].astype(jnp.bfloat16))
            x = shift(send, [(0, 1), (1, 0), (2, 3), (3, 2)])
            came[c].append((x, 0))
            came[other].append((x, 1))
            near = (own + jnp.where(is_outer, 0.0, x.astype(jnp.float32))).astype(jnp.bfloat16)
        else:
            for k in range(right - 1):
                came[c].append((shift(near, [(k, k + 1), (rows - 1 - k, rows - 2 - k)]), None))
                near = (own + sum(x.astype(jnp.float32) for x, _ in came[c])).astype(jnp.bfloat16)
        mid = shift(near, [(right - 1, right), (right, right - 1)])
        came[c].append((mid, None))
        outs.append(own + mid.astype(jnp.float32))
    for c, out in enumerate(outs):
        if c in joined.values():
            continue
        for k in reversed(range(right - 1)):
            send = out.astype(jnp.bfloat16)
            far = shift(send, [(k + 1, k), (rows - 2 - k, rows - 1 - k)])
            came[c].append((far, None))
            out = out + far.astype(jnp.float32)
    sums = [(own, part) for (own, _), part in zip(owns, came)]
    state = grads = None
    late = []
    for c, (first, count) in enumerate(plan):
        whole_chunk = c + LATE < len(plan)
        *state, one, two = chunk_kernel(
            *sums[c], flags, up_weight, mu, state, grads, weights if whole_chunk else None, first, count, width
        )
        if whole_chunk:
            grads = [one, two]
        else:
            late.append((c, first, count, one, two))
    for c, first, count, act, hgrad in late:
        grads = weight_grads(act, hgrad, mu, weights, grads, units, first, count, width)
    input_grad = scatter_tokens(*state, cols)
    return (input_grad.astype(jnp.bfloat16), *grads)


def whole(rows, cols, *arrays):
    return local(rows, cols, *arrays)


def solution(mesh):
    return jax.shard_map(
        functools.partial(whole, mesh.shape["row"], mesh.shape["col"]),
        mesh=mesh,
        in_specs=(P("col", "row"), P("col", "row"), P("row", "col"), P("col", "row"), P()),
        out_specs=(P("col", "row"), P("row", "col"), P("col", "row")),
        check_vma=False,
    )
```
